32 devices in a mesh: slab: 8 (over y, x, core), grp: 4 (over z).
Axes of the slice: x: 2, y: 2, z: 4, core: 2. Of those that a mesh axis runs over, the one named last changes fastest.
Arguments:
- volume: float32 [64, 32, 16, 128], P(None, 'slab', 'grp'), may hold values from -6 to 6
- conv_fine: float32 [3, 3, 3, 64, 64], replicated, may hold values from -0.15625 to 0.15625
- down_first: float32 [2, 2, 2, 64, 128], replicated, may hold values from -0.25 to 0.25
- conv_middle: float32 [3, 3, 3, 128, 128], replicated, may hold values from -0.109375 to 0.109375
- down_second: float32 [2, 2, 2, 128, 256], P(None, None, None, None, 'grp'), may hold values from -0.1875 to 0.1875
- conv_coarse: float32 [3, 3, 3, 256, 512], P(None, None, None, None, 'grp'), may hold values from -0.078125 to 0.078125
Outputs:
- features: float32 [512, 8, 128], P('grp', 'slab')
The draws below stay inside these ranges and needn't reach their ends.
All inputs are finite; a program needn't handle non-finite values.
Results may differ from the reference program's by a relative error of at most 0.000082.
Values sent between devices are 32-bit elements; how exact they have to be, the bound alone decides.
A program may use at most 64 MiB of HBM per device.

```python
import jax
import jax.numpy as jnp
from jax import lax

C1 = 64
C2 = 128
C3 = 256
C4 = 512
WIDTH = 128
DEPTH = 32
HEIGHT = 16


def shard_levels(key, dims, pieces, low, largest):
    factor_of = 1.0
    for dim, parts in pieces:
        steps = jax.random.uniform(jax.random.fold_in(jax.random.fold_in(key, 6), dim), (parts,), jnp.float32, low / len(pieces), largest / len(pieces))
        factor_of = factor_of * jnp.repeat(jnp.exp(steps), dims[dim] // parts).reshape((-1,) + (1,) * (len(dims) - 1 - dim))
    return factor_of


def scatter_about(own_key, extent, deviation, reach, pieces=(), dtype=jnp.bfloat16):
    values = deviation * jax.random.normal(own_key, extent, jnp.float32)
    if pieces:
        values = values * shard_levels(own_key, extent, pieces, -0.22, 0.18)
    return jnp.clip(values, -reach, reach).astype(dtype)


def setup_inputs(seed: int = 0) -> dict:
    keys = jax.random.split(jax.random.key(seed), 7)
    volume = scatter_about(keys[0], (C1, DEPTH, HEIGHT, WIDTH), 1.0, 6.0, ((1, 8), (2, 4)), jnp.float32)
    conv_fine = scatter_about(keys[1], (3, 3, 3, C1, C1), (27 * C1) ** -0.5, 0.15625, (), jnp.float32)
    down_first = scatter_about(keys[2], (2, 2, 2, C1, C2), (8 * C1) ** -0.5, 0.25, (), jnp.float32)
    conv_middle = scatter_about(keys[3], (3, 3, 3, C2, C2), (27 * C2) ** -0.5, 0.109375, (), jnp.float32)
    down_second = scatter_about(keys[4], (2, 2, 2, C2, C3), (8 * C2) ** -0.5, 0.1875, ((4, 4),), jnp.float32)
    conv_coarse = scatter_about(keys[5], (3, 3, 3, C3, C4), (27 * C3) ** -0.5, 0.078125, ((4, 4),), jnp.float32)
    return {"volume": volume, "conv_fine": conv_fine, "down_first": down_first, "conv_middle": conv_middle, "down_second": down_second, "conv_coarse": conv_coarse}


def convolve(field, kernel, stride, padding):
    return lax.conv_general_dilated(field[None], kernel, (stride, stride, stride), padding, dimension_numbers=("NCDHW", "DHWIO", "NCDHW"), precision=lax.Precision.HIGHEST)[0]


def reference(volume, conv_fine, down_first, conv_middle, down_second, conv_coarse):
    same = ((1, 1), (1, 1), (1, 1))
    valid = ((0, 0), (0, 0), (0, 0))
    level_one = jax.nn.gelu(convolve(volume, conv_fine, 1, same), approximate=False)
    level_two = convolve(level_one, down_first, 2, valid)
    level_two = jax.nn.gelu(convolve(level_two, conv_middle, 1, same), approximate=False)
    coarse = convolve(level_two, down_second, 2, valid)
    result = jax.nn.gelu(convolve(coarse, conv_coarse, 1, same), approximate=False)
    return result.reshape(C4, DEPTH // 4, (HEIGHT // 4) * (WIDTH // 4))
```

```python
import jax
import jax.numpy as jnp
from jax import lax
from jax.sharding import PartitionSpec as P


def padded_2(cells, sides, width):
    for axis, dim in sides:
        count = lax.axis_size(axis)
        ends = count - 1
        head = lax.slice_in_dim(cells, 0, width, axis=dim)
        tail = lax.slice_in_dim(cells, cells.shape[dim] - width, cells.shape[dim], axis=dim)
        cells = jnp.concatenate(
            [
                lax.ppermute(tail, axis, [(i, (i + 1) % count) for i in range(ends)]),
                cells,
                lax.ppermute(head, axis, [((i + 1) % count, i) for i in range(ends)]),
            ],
            axis=dim,
        )
    return cells


def from_behind(shard, axis, by):
    peers = lax.axis_size(axis)
    pairs = [(i, i + by) for i in range(peers) if 0 <= i + by < peers]
    return lax.ppermute(shard, axis, pairs)


def convolve(field, kernel, stride, padding):
    return lax.conv_general_dilated(
        field[None],
        kernel,
        (stride, stride, stride),
        padding,
        dimension_numbers=("NCDHW", "DHWIO", "NCDHW"),
        precision=lax.Precision.HIGH,
    )[0]


def per_device(volume, conv_fine, down_first, conv_middle, down_second, conv_coarse):
    valid = ((0, 0), (0, 0), (0, 0))
    sideways = ((0, 0), (0, 0), (1, 1))
    padded = padded_2(volume, (("slab", 1), ("grp", 2)), 1)
    level_one = jax.nn.gelu(convolve(padded, conv_fine, 1, sideways), approximate=False)
    level_two = convolve(level_one, down_first, 2, valid)
    padded_two = padded_2(level_two, (("slab", 1), ("grp", 2)), 1)
    level_two = jax.nn.gelu(convolve(padded_two, conv_middle, 1, sideways), approximate=False)
    gathered = lax.all_gather(level_two, "grp", axis=2, tiled=True)
    shares = convolve(gathered, down_second, 2, valid)
    coarse = lax.all_gather(shares, "grp", axis=0, tiled=True)
    planar = ((0, 0), (1, 1), (1, 1))
    summed = convolve(coarse, conv_coarse, 1, ((1, 1), (1, 1), (1, 1)))
    upward = convolve(coarse[:, -1:], conv_coarse[0:1], 1, planar)
    downward = convolve(coarse[:, :1], conv_coarse[2:3], 1, planar)
    from_lower = from_behind(upward, "slab", 1)
    from_upper = from_behind(downward, "slab", -1)
    summed = summed.at[:, :1].add(from_lower)
    summed = summed.at[:, -1:].add(from_upper)
    result = jax.nn.gelu(summed, approximate=False)
    return result.reshape(result.shape[0], result.shape[1], result.shape[2] * result.shape[3])


def solution(mesh):
    placed = (
        P(None, "slab", "grp", None),
        P(),
        P(),
        P(),
        P(None, None, None, None, "grp"),
        P(None, None, None, None, "grp"),
    )
    return jax.shard_map(
        per_device, mesh=mesh, in_specs=placed, out_specs=P("grp", "slab", None), check_vma=False
    )
```

```python
import functools

import jax
import jax.numpy as jnp
from jax import lax
from jax.experimental import pallas as pl
from jax.experimental.pallas import tpu as pltpu
from jax.sharding import PartitionSpec as P

MESH = pl.DeviceIdType.MESH
F32, BF16 = jnp.float32, jnp.bfloat16
WAYS = ((1, 0), (-1, 0), (0, 1), (0, -1), (1, 1), (1, -1), (-1, 1), (-1, -1))


def split(x):
    high = x.astype(BF16)
    return high, (x - high.astype(F32)).astype(BF16)


def dot3(a, b, dims=(((1,), (0,)), ((), ()))):
    dot = functools.partial(lax.dot_general, dimension_numbers=dims, preferred_element_type=F32)
    return dot(a[0], b[0]) + dot(a[1], b[0]) + dot(a[0], b[1])


def gelu(x):
    return 0.5 * x * (1.0 + lax.erf(x * (0.5**0.5)))


def beside(x, span):
    at = lax.rem(lax.broadcasted_iota(jnp.int32, x.shape, 0), span)
    before = jnp.where(at == 0, 0.0, pltpu.roll(x, 1, 0))
    after = jnp.where(at == span - 1, 0.0, pltpu.roll(x, x.shape[0] - 1, 0))
    return before, after


def kernel(
    slabs, groups,
    vol, fine, down1_hbm, middle_hbm, shard, coarse_hbm,
    out,
    field, pair, rows_h, rows_l, fine_h, fine_l, down1, middle, middle_h, middle_l,
    second, rows2_h, rows2_l, level2, gathered, coarse_w, coarse_h, coarse_l,
    coarse, taps_h, taps_l, upward, downward, from_lower, from_upper,
    load_sem, send1, recv1, send2, recv2, wsend, wrecv, fsend, frecv, csend, crecv, psend, precv,
):
    s, g = lax.axis_index("slab"), lax.axis_index("grp")
    depth, height, chans, width = vol.shape
    half = width // 2

    loads = [
        pltpu.make_async_copy(down1_hbm, down1, load_sem.at[0]),
        pltpu.make_async_copy(middle_hbm, middle, load_sem.at[1]),
        pltpu.make_async_copy(coarse_hbm, coarse_w, load_sem.at[2]),
    ]
    for load in loads:
        load.start()

    def exists(ds, dg):
        return (s + ds >= 0) & (s + ds < slabs) & (g + dg >= 0) & (g + dg < groups)

    barrier = pltpu.get_barrier_semaphore()
    heard = jnp.int32(0)
    for ds, dg in WAYS:
        there = exists(ds, dg)
        heard = heard + there.astype(jnp.int32)

        @pl.when(there)
        def _():
            pl.semaphore_signal(barrier, inc=1, device_id=(s + ds, g + dg), device_id_type=MESH)

    for dg in range(2, groups):
        for sign in (1, -1):
            there = exists(0, sign * dg)
            heard = heard + there.astype(jnp.int32)

            @pl.when(there)
            def _():
                pl.semaphore_signal(barrier, inc=1, device_id=(s, g + sign * dg), device_id_type=MESH)

    pl.semaphore_wait(barrier, heard)

    def part(way, size, offset):
        if way == 0:
            return pl.ds(offset, size)
        return pl.ds(offset + (size - 1 if way > 0 else 0), 1)

    def landing(way, size):
        if way == 0:
            return pl.ds(1, size)
        return pl.ds(0 if way > 0 else size + 1, 1)

    def halo(src, offset, buf, sends, recvs):
        nd, nh = buf.shape[0] - 2, buf.shape[1] - 2
        copies = []
        for k, (ds, dg) in enumerate(WAYS):
            copies.append(
                pltpu.make_async_remote_copy(
                    src_ref=src.at[part(ds, nd, offset), part(dg, nh, offset)],
                    dst_ref=buf.at[landing(ds, nd), landing(dg, nh)],
                    send_sem=sends.at[k],
                    recv_sem=recvs.at[k],
                    device_id=(s + ds, g + dg),
                    device_id_type=MESH,
                )
            )

            @pl.when(exists(ds, dg))
            def _():
                copies[k].start()

            @pl.when(jnp.logical_not(exists(-ds, -dg)))
            def _():
                piece = (landing(ds, nd), landing(dg, nh))
                shape = (piece[0].size, piece[1].size) + buf.shape[2:]
                buf[piece[0], piece[1]] = jnp.zeros(shape, F32)

        return copies

    def arrive(copies, received):
        for k, (ds, dg) in enumerate(WAYS):
            if received:
                @pl.when(exists(-ds, -dg))
                def _():
                    copies[k].wait_recv()
            else:
                @pl.when(exists(ds, dg))
                def _():
                    copies[k].wait_send()

    first = halo(vol, 0, field, send1, recv1)

    part_rows = shard.shape[0] // 2
    mine = pl.ds(pl.multiple_of(lax.rem(s, 2) * part_rows, part_rows), part_rows)
    sibling = s + 1 - 2 * lax.rem(s, 2)
    spread = []
    for j in range(1, groups):
        copy = pltpu.make_async_remote_copy(
            src_ref=shard.at[mine],
            dst_ref=gathered.at[g, mine],
            send_sem=wsend.at[j],
            recv_sem=wrecv.at[j],
            device_id=(s, lax.rem(g + j, groups)),
            device_id_type=MESH,
        )
        copy.start()
        spread.append(copy)
    gathered[pl.ds(g, 1)] = shard[...][None]

    blank = jnp.zeros((chans, 2 * chans), BF16)
    nothing = jnp.zeros((chans, chans), F32)
    for a in range(3):
        for b in range(3):
            for pos in range(4):
                left = fine[(a * 3 + b) * 3 + pos] if pos < 3 else nothing
                right = fine[(a * 3 + b) * 3 + pos - 1] if pos > 0 else nothing
                high, low = split(jnp.concatenate([left, right], axis=1))
                for hb in range(2):
                    p, sub = divmod(b + hb, 2)
                    spot = pl.ds((pos * 2 + sub) * chans, chans)
                    fine_h[a, p, spot, hb * 2 * chans : (hb + 1) * 2 * chans] = high
                    fine_l[a, p, spot, hb * 2 * chans : (hb + 1) * 2 * chans] = low
        for pos in range(4):
            for p, sub, hb in ((0, 0, 1), (1, 1, 0)):
                spot = pl.ds((pos * 2 + sub) * chans, chans)
                fine_h[a, p, spot, hb * 2 * chans : (hb + 1) * 2 * chans] = blank
                fine_l[a, p, spot, hb * 2 * chans : (hb + 1) * 2 * chans] = blank

    loads[1].wait()

    @pl.loop(0, 9)
    def _(t):
        middle_h[t], middle_l[t] = split(middle[t])

    field[1 : depth + 1, 1 : height + 1] = vol[...]
    arrive(first, True)

    pairs = height // 2 + 1

    @pl.loop(0, depth + 2)
    def _(d):
        for p in range(pairs):
            both = field[d, 2 * p : 2 * p + 2].reshape(2 * chans, width)
            pair[p] = both.T
        for p in range(pairs):
            even = pair[p, pl.ds(0, half, stride=2), :]
            odd = pair[p, pl.ds(1, half, stride=2), :]
            before, _ = beside(odd, half)
            _, after = beside(even, half)
            rows_h[d, p], rows_l[d, p] = split(jnp.concatenate([before, even, odd, after], axis=1))

    blocks = height // 2
    total = None
    for a in range(3):
        for p in range(2):
            lhs = [
                r[a : a + depth, p : p + blocks].reshape(depth * blocks * half, 8 * chans) for r in (rows_h, rows_l)
            ]
            term = dot3(lhs, (fine_h[a, p], fine_l[a, p]))
            total = term if total is None else total + term
    one = gelu(total).reshape(depth // 2, 2, blocks * half, 4 * chans)
    loads[0].wait()
    total = None
    for a in range(2):
        lhs = one[:, a].reshape(depth // 2 * blocks * half, 4 * chans)
        term = dot3(split(lhs), split(down1[a]))
        total = term if total is None else total + term
    d2, h2, c2 = depth // 2, blocks, total.shape[1]
    second[1 : d2 + 1, 1 : h2 + 1] = total.reshape(d2, h2, half, c2)
    again = halo(second, 1, second, send2, recv2)

    forward = []
    for j in range(1, groups):
        spread[j - 1].wait_recv()
        source = lax.rem(g + groups - j, groups)
        copy = pltpu.make_async_remote_copy(
            src_ref=gathered.at[source, mine],
            dst_ref=gathered.at[source, mine],
            send_sem=fsend.at[j],
            recv_sem=frecv.at[j],
            device_id=(sibling, g),
            device_id_type=MESH,
        )
        copy.start()
        forward.append(copy)

    loads[2].wait()

    @pl.loop(0, 9)
    def _(t):
        coarse_h[t], coarse_l[t] = split(coarse_w[t])

    arrive(again, True)

    @pl.loop(0, d2 + 2)
    def _(d):
        for h in range(h2 + 2):
            x = second[d, h]
            before, after = beside(x, half)
            rows2_h[d, h], rows2_l[d, h] = split(jnp.concatenate([before, x, after], axis=1))

    total = None
    for a in range(3):
        for b in range(3):
            lhs = [r[a : a + d2, b : b + h2].reshape(d2 * h2 * half, 3 * c2) for r in (rows2_h, rows2_l)]
            term = dot3(lhs, (middle_h[a * 3 + b], middle_l[a * 3 + b]))
            total = term if total is None else total + term
    level2[...] = gelu(total)
    quarter = half // 2
    lhs = jnp.concatenate(
        [level2[pl.ds(r * half + c, quarter, stride=2), :] for r in range(d2 * h2) for c in range(2)], axis=1
    )
    for copy in forward:
        copy.wait_recv()
    weights = gathered[...].reshape(groups * shard.shape[0], shard.shape[1])
    share = dot3(split(lhs), split(weights), (((1,), (1,)), ((), ())))
    coarse[pl.ds(g, 1)] = share[None]
    sent = []
    for j in range(1, groups):
        copy = pltpu.make_async_remote_copy(
            src_ref=coarse.at[g],
            dst_ref=coarse.at[g],
            send_sem=csend.at[j],
            recv_sem=crecv.at[j],
            device_id=(s, lax.rem(g + j, groups)),
            device_id_type=MESH,
        )
        copy.start()
        sent.append(copy)
    cells = groups * quarter
    edge = jnp.zeros((quarter, taps_h.shape[1]), BF16)
    for taps in (taps_h, taps_l):
        taps[0:quarter] = edge
        taps[quarter + cells : 2 * quarter + cells] = edge
    for copy in sent:
        copy.wait_recv()
    x = coarse[...].reshape(cells, coarse.shape[2])
    before, after = beside(x, quarter)
    high, low = split(jnp.concatenate([before, x, after], axis=1))
    taps_h[quarter : quarter + cells] = high
    taps_l[quarter : quarter + cells] = low

    def plane(a):
        total = None
        for b in range(3):
            lhs = [t[b * quarter : b * quarter + cells] for t in (taps_h, taps_l)]
            term = dot3(lhs, (coarse_h[a * 3 + b], coarse_l[a * 3 + b]))
            total = term if total is None else total + term
        return total

    upward[...] = plane(0)
    up = pltpu.make_async_remote_copy(
        src_ref=upward, dst_ref=from_lower, send_sem=psend.at[0], recv_sem=precv.at[0],
        device_id=(s + 1, g), device_id_type=MESH,
    )
    down = pltpu.make_async_remote_copy(
        src_ref=downward, dst_ref=from_upper, send_sem=psend.at[1], recv_sem=precv.at[1],
        device_id=(s - 1, g), device_id_type=MESH,
    )

    @pl.when(exists(1, 0))
    def _():
        up.start()

    @pl.when(jnp.logical_not(exists(-1, 0)))
    def _():
        from_lower[...] = jnp.zeros(from_lower.shape, F32)

    downward[...] = plane(2)

    @pl.when(exists(-1, 0))
    def _():
        down.start()

    @pl.when(jnp.logical_not(exists(1, 0)))
    def _():
        from_upper[...] = jnp.zeros(from_upper.shape, F32)

    centre = plane(1)

    @pl.when(exists(-1, 0))
    def _():
        up.wait_recv()

    @pl.when(exists(1, 0))
    def _():
        down.wait_recv()

    out[...] = gelu(centre + from_lower[...] + from_upper[...]).T

    arrive(first, False)
    arrive(again, False)
    for copy in spread + forward + sent:
        copy.wait_send()

    @pl.when(exists(1, 0))
    def _():
        up.wait_send()

    @pl.when(exists(-1, 0))
    def _():
        down.wait_send()


def per_device(slabs, groups, volume, conv_fine, down_first, conv_middle, down_second, conv_coarse):
    c1, depth, height, width = volume.shape
    c2, c3, c4 = down_first.shape[4], conv_coarse.shape[3], conv_coarse.shape[4]
    half, quarter = width // 2, width // 4
    d2, h2 = depth // 2, height // 2
    part = down_second.shape[4]
    cells = groups * quarter
    vol = jnp.transpose(volume, (1, 2, 0, 3))
    fine = conv_fine.reshape(27, c1, c1)
    down1 = down_first.reshape(2, 4 * c1, c2)
    middle = conv_middle.reshape(9, 3 * c2, c2)
    shard = down_second.reshape(8 * c2, part).T
    coarse_w = conv_coarse.reshape(9, 3 * c3, c4)
    V = pltpu.VMEM
    vmem, away = pl.BlockSpec(memory_space=pltpu.VMEM), pl.BlockSpec(memory_space=pl.ANY)
    dma = pltpu.SemaphoreType.DMA
    result = pl.pallas_call(
        functools.partial(kernel, slabs, groups),
        out_shape=jax.ShapeDtypeStruct((c4, cells), F32),
        in_specs=[vmem, vmem, away, away, vmem, away],
        out_specs=vmem,
        scratch_shapes=[
            V((depth + 2, height + 2, c1, width), F32),
            V((h2 + 1, width, 2 * c1), F32),
            V((depth + 2, h2 + 1, half, 8 * c1), BF16),
            V((depth + 2, h2 + 1, half, 8 * c1), BF16),
            V((3, 2, 8 * c1, 4 * c1), BF16),
            V((3, 2, 8 * c1, 4 * c1), BF16),
            V(down1.shape, F32),
            V(middle.shape, F32),
            V(middle.shape, BF16),
            V(middle.shape, BF16),
            V((d2 + 2, h2 + 2, half, c2), F32),
            V((d2 + 2, h2 + 2, half, 3 * c2), BF16),
            V((d2 + 2, h2 + 2, half, 3 * c2), BF16),
            V((d2 * h2 * half, c2), F32),
            V((groups,) + shard.shape, F32),
            V(coarse_w.shape, F32),
            V(coarse_w.shape, BF16),
            V(coarse_w.shape, BF16),
            V((groups, quarter, c3), F32),
            V((cells + 2 * quarter, 3 * c3), BF16),
            V((cells + 2 * quarter, 3 * c3), BF16),
            V((cells, c4), F32),
            V((cells, c4), F32),
            V((cells, c4), F32),
            V((cells, c4), F32),
            dma((3,)),
            dma((8,)), dma((8,)), dma((8,)), dma((8,)),
            dma((groups,)), dma((groups,)), dma((groups,)), dma((groups,)), dma((groups,)), dma((groups,)),
            dma((2,)), dma((2,)),
        ],
        compiler_params=pltpu.CompilerParams(
            collective_id=0, has_side_effects=True, vmem_limit_bytes=60 * 1024 * 1024
        ),
    )(vol, fine, down1, middle, shard, coarse_w)
    return result.reshape(c4, 1, cells)


def solution(mesh):
    placed = (
        P(None, "slab", "grp", None),
        P(),
        P(),
        P(),
        P(None, None, None, None, "grp"),
        P(None, None, None, None, "grp"),
    )
    body = functools.partial(per_device, mesh.shape["slab"], mesh.shape["grp"])
    return jax.shard_map(
        body, mesh=mesh, in_specs=placed, out_specs=P("grp", "slab", None), check_vma=False
    )
```

```python
import functools

import jax
import jax.numpy as jnp
from jax import lax
from jax.experimental import pallas as pl
from jax.experimental.pallas import tpu as pltpu
from jax.sharding import PartitionSpec as P

MESH = pl.DeviceIdType.MESH
F32, BF16 = jnp.float32, jnp.bfloat16
WAYS = ((1, 0), (-1, 0), (0, 1), (0, -1), (1, 1), (1, -1), (-1, 1), (-1, -1))


def split(x):
    high = x.astype(BF16)
    return high, (x - high.astype(F32)).astype(BF16)


def stacked(x):
    return jnp.concatenate(split(x), axis=0)


def product(both, weights, dims=(((1,), (0,)), ((), ()))):
    dot = functools.partial(lax.dot_general, dimension_numbers=dims, preferred_element_type=F32)
    rows = both.shape[0] // 2
    wide = dot(both, weights[0])
    return wide[:rows] + wide[rows:] + dot(both[:rows], weights[1])


def plus(total, term):
    return term if total is None else total + term


def gelu(x):
    return 0.5 * x * (1.0 + lax.erf(x * (0.5**0.5)))


def beside(x, span):
    at = lax.rem(lax.broadcasted_iota(jnp.int32, x.shape, 0), span)
    before = jnp.where(at == 0, 0.0, pltpu.roll(x, 1, 0))
    after = jnp.where(at == span - 1, 0.0, pltpu.roll(x, x.shape[0] - 1, 0))
    return before, after


def kernel(
    slabs, groups,
    vol, fine, down1_hbm, middle_hbm, shard, coarse_hbm,
    out,
    field, pair, rows, fine_h, fine_l, down1, down1_h, down1_l, middle, middle_h, middle_l,
    second, rows2, level2, gathered, coarse_w, edges_h, edges_l, centre_h, centre_l,
    coarse, taps, upward, downward, from_lower, from_upper,
    load_sem, send1, recv1, send2, recv2, wsend, wrecv, xsend, xrecv, fsend, frecv, csend, crecv, psend, precv,
):
    s, g = lax.axis_index("slab"), lax.axis_index("grp")
    depth, height, chans, width = (field.shape[0] - 2, field.shape[1] - 2) + field.shape[2:]
    half = width // 2

    loads = [
        pltpu.make_async_copy(down1_hbm, down1, load_sem.at[0]),
        pltpu.make_async_copy(middle_hbm, middle, load_sem.at[1]),
        pltpu.make_async_copy(coarse_hbm, coarse_w, load_sem.at[2]),
    ]
    for load in loads:
        load.start()

    def exists(ds, dg):
        return (s + ds >= 0) & (s + ds < slabs) & (g + dg >= 0) & (g + dg < groups)

    lines = depth * height
    for r in range(lines):
        field[1 + r // height, 1 + r % height] = vol[pl.ds(r, chans, stride=lines), :]

    barrier = pltpu.get_barrier_semaphore()
    heard = jnp.int32(0)
    for ds, dg in WAYS:
        there = exists(ds, dg)
        heard = heard + there.astype(jnp.int32)

        @pl.when(there)
        def _():
            pl.semaphore_signal(barrier, inc=1, device_id=(s + ds, g + dg), device_id_type=MESH)

    for dg in range(2, groups):
        for sign in (1, -1):
            there = exists(0, sign * dg)
            heard = heard + there.astype(jnp.int32)

            @pl.when(there)
            def _():
                pl.semaphore_signal(barrier, inc=1, device_id=(s, g + sign * dg), device_id_type=MESH)

    sibling = s + 1 - 2 * lax.rem(s, 2)
    across = s + 2 - 4 * lax.rem(s // 2, 2)
    pl.semaphore_signal(barrier, inc=1, device_id=(across, g), device_id_type=MESH)
    pl.semaphore_wait(barrier, heard + 1)

    def part(way, size, offset):
        if way == 0:
            return pl.ds(offset, size)
        return pl.ds(offset + (size - 1 if way > 0 else 0), 1)

    def landing(way, size):
        if way == 0:
            return pl.ds(1, size)
        return pl.ds(0 if way > 0 else size + 1, 1)

    def halo(src, offset, buf, sends, recvs):
        nd, nh = buf.shape[0] - 2, buf.shape[1] - 2
        copies = []
        for k, (ds, dg) in enumerate(WAYS):
            copies.append(
                pltpu.make_async_remote_copy(
                    src_ref=src.at[part(ds, nd, offset), part(dg, nh, offset)],
                    dst_ref=buf.at[landing(ds, nd), landing(dg, nh)],
                    send_sem=sends.at[k],
                    recv_sem=recvs.at[k],
                    device_id=(s + ds, g + dg),
                    device_id_type=MESH,
                )
            )

            @pl.when(exists(ds, dg))
            def _():
                copies[k].start()

            @pl.when(jnp.logical_not(exists(-ds, -dg)))
            def _():
                piece = (landing(ds, nd), landing(dg, nh))
                shape = (piece[0].size, piece[1].size) + buf.shape[2:]
                buf[piece[0], piece[1]] = jnp.zeros(shape, F32)

        return copies

    def arrive(copies, received, ways=range(len(WAYS))):
        for k in ways:
            ds, dg = WAYS[k]
            if received:
                @pl.when(exists(-ds, -dg))
                def _():
                    copies[k].wait_recv()
            else:
                @pl.when(exists(ds, dg))
                def _():
                    copies[k].wait_send()

    first = halo(field, 1, field, send1, recv1)

    taps_of = shard.shape[0]
    parity, bit = lax.rem(s, 2), lax.rem(s // 2, 2)
    quarter_taps = pl.ds((parity * 2 + bit) * (taps_of // 4), taps_of // 4)
    half_taps = pl.ds(parity * (taps_of // 2), taps_of // 2)
    spread, crossed, forward = [], [], []
    for j in range(1, groups):
        copy = pltpu.make_async_remote_copy(
            src_ref=shard.at[quarter_taps],
            dst_ref=gathered.at[g, quarter_taps],
            send_sem=wsend.at[j],
            recv_sem=wrecv.at[j],
            device_id=(s, lax.rem(g + j, groups)),
            device_id_type=MESH,
        )
        copy.start()
        spread.append(copy)

    def hand_on(arrived, out_copies, piece, sends, recvs, peer):
        for j in range(1, groups):
            arrived[j - 1].wait_recv()
            source = lax.rem(g + groups - j, groups)
            copy = pltpu.make_async_remote_copy(
                src_ref=gathered.at[source, piece],
                dst_ref=gathered.at[source, piece],
                send_sem=sends.at[j],
                recv_sem=recvs.at[j],
                device_id=(peer, g),
                device_id_type=MESH,
            )
            copy.start()
            out_copies.append(copy)

    gathered[pl.ds(g, 1)] = shard[...][None]

    blank = jnp.zeros((chans, 2 * chans), BF16)
    nothing = jnp.zeros((chans, chans), F32)
    for a in range(3):
        for b in range(3):
            for pos in range(4):
                left = fine[(a * 3 + b) * 3 + pos] if pos < 3 else nothing
                right = fine[(a * 3 + b) * 3 + pos - 1] if pos > 0 else nothing
                high, low = split(jnp.concatenate([left, right], axis=1))
                for hb in range(2):
                    p, sub = divmod(b + hb, 2)
                    spot = pl.ds((pos * 2 + sub) * chans, chans)
                    fine_h[a, p, spot, hb * 2 * chans : (hb + 1) * 2 * chans] = high
                    fine_l[a, p, spot, hb * 2 * chans : (hb + 1) * 2 * chans] = low
        for pos in range(4):
            for p, sub, hb in ((0, 0, 1), (1, 1, 0)):
                spot = pl.ds((pos * 2 + sub) * chans, chans)
                fine_h[a, p, spot, hb * 2 * chans : (hb + 1) * 2 * chans] = blank
                fine_l[a, p, spot, hb * 2 * chans : (hb + 1) * 2 * chans] = blank

    pairs = height // 2 + 1
    blocks = height // 2
    d2, h2, c2 = depth // 2, blocks, down1.shape[2]
    for load in loads:
        load.wait()
    for a in range(2):
        down1_h[a], down1_l[a] = split(down1[a])

    @pl.loop(0, 3)
    def _(a):
        for b in range(3):
            high, low = split(middle[a * 3 + b])
            for hb in range(2):
                spot = pl.ds((b + hb) * 3 * c2, 3 * c2)
                middle_h[a, spot, hb * c2 : (hb + 1) * c2] = high
                middle_l[a, spot, hb * c2 : (hb + 1) * c2] = low

    outs = coarse_w.shape[2]

    @pl.loop(0, 3)
    def _(b):
        for a, k in ((0, 0), (2, 1)):
            high, low = split(coarse_w[a * 3 + b])
            edges_h[b, :, k * outs : (k + 1) * outs] = high
            edges_l[b, :, k * outs : (k + 1) * outs] = low
        centre_h[b], centre_l[b] = split(coarse_w[3 + b])

    def build(p):
        @pl.loop(0, depth + 2)
        def _(d):
            pair[p] = field[d, 2 * p : 2 * p + 2].reshape(2 * chans, width).T
            even = pair[p, pl.ds(0, half, stride=2), :]
            odd = pair[p, pl.ds(1, half, stride=2), :]
            before, _ = beside(odd, half)
            _, after = beside(even, half)
            rows[0, d, p], rows[1, d, p] = split(jnp.concatenate([before, even, odd, after], axis=1))

    totals = [None] * blocks

    def convolve(p):
        for a in range(3):
            lhs = rows[:, a : a + depth, p].reshape(2 * depth * half, 8 * chans)
            for block in range(blocks):
                if 0 <= p - block <= 1:
                    w = (fine_h[a, p - block], fine_l[a, p - block])
                    totals[block] = plus(totals[block], product(lhs, w))

    arrive(first, True, range(0, 2))
    for p in range(1, blocks):
        build(p)
        convolve(p)
    arrive(first, True, range(2, len(WAYS)))
    for p in (0, blocks):
        build(p)
        convolve(p)
    ones = [gelu(t).reshape(d2, 2, half, 4 * chans) for t in totals]
    total = None
    for a in range(2):
        lhs = jnp.concatenate([o[:, a].reshape(d2 * half, 4 * chans) for o in ones], axis=0)
        total = plus(total, product(stacked(lhs), (down1_h[a], down1_l[a])))
    total = total.reshape(h2, d2, half, c2)
    for h in range(h2):
        second[1 : d2 + 1, 1 + h] = total[h]
    again = halo(second, 1, second, send2, recv2)
    hand_on(spread, crossed, quarter_taps, xsend, xrecv, across)

    def widen(h):
        @pl.loop(0, d2 + 2)
        def _(d):
            x = second[d, h]
            before, after = beside(x, half)
            spot = slice(h * 3 * c2, (h + 1) * 3 * c2)
            rows2[0, d, :, spot], rows2[1, d, :, spot] = split(jnp.concatenate([before, x, after], axis=1))

    def middle_term(a, low, high, left, right):
        lhs = rows2[:, a : a + d2, :, low:high].reshape(2 * d2 * half, high - low)
        return product(lhs, (middle_h[a, low:high, left:right], middle_l[a, low:high, left:right]))

    k3 = 3 * c2
    arrive(again, True, range(0, 2))
    for h in range(1, h2 + 1):
        widen(h)
    total, sides = None, [None, None]
    for a in range(3):
        total = plus(total, middle_term(a, k3, 3 * k3, 0, 2 * c2))
    arrive(again, True, range(2, len(WAYS)))
    for h in (0, h2 + 1):
        widen(h)
    for a in range(3):
        sides[0] = plus(sides[0], middle_term(a, 0, k3, 0, c2))
        sides[1] = plus(sides[1], middle_term(a, 3 * k3, 4 * k3, c2, 2 * c2))
    hand_on(crossed, forward, half_taps, fsend, frecv, sibling)
    for h in range(h2):
        level2[h] = gelu(total[:, h * c2 : (h + 1) * c2] + sides[h])
    quarter = half // 2
    lhs = jnp.concatenate(
        [
            level2[h, pl.ds(d * half + c, quarter, stride=2), :]
            for d in range(d2) for h in range(h2) for c in range(2)
        ],
        axis=1,
    )
    lhs = stacked(lhs)
    for copy in forward:
        copy.wait_recv()
    weights = jnp.concatenate(
        [gathered[:, t].reshape(groups * shard.shape[1], c2) for t in range(taps_of)], axis=1
    )
    share = product(lhs, split(weights), (((1,), (1,)), ((), ())))
    coarse[pl.ds(g, 1)] = share[None]
    sent = []
    for j in range(1, groups):
        copy = pltpu.make_async_remote_copy(
            src_ref=coarse.at[g],
            dst_ref=coarse.at[g],
            send_sem=csend.at[j],
            recv_sem=crecv.at[j],
            device_id=(s, lax.rem(g + j, groups)),
            device_id_type=MESH,
        )
        copy.start()
        sent.append(copy)
    cells = groups * quarter
    edge = jnp.zeros((2, quarter, taps.shape[2]), BF16)
    taps[:, 0:quarter] = edge
    taps[:, quarter + cells : 2 * quarter + cells] = edge
    for copy in sent:
        copy.wait_recv()
    x = coarse[...].reshape(cells, coarse.shape[2])
    before, after = beside(x, quarter)
    taps[0, quarter : quarter + cells], taps[1, quarter : quarter + cells] = split(
        jnp.concatenate([before, x, after], axis=1)
    )

    def plane(high, low):
        total = None
        for b in range(3):
            lhs = taps[:, b * quarter : b * quarter + cells].reshape(2 * cells, taps.shape[2])
            total = plus(total, product(lhs, (high[b], low[b])))
        return total

    both = plane(edges_h, edges_l)
    upward[...] = both[:, :outs]
    downward[...] = both[:, outs:]
    up = pltpu.make_async_remote_copy(
        src_ref=upward, dst_ref=from_lower, send_sem=psend.at[0], recv_sem=precv.at[0],
        device_id=(s + 1, g), device_id_type=MESH,
    )
    down = pltpu.make_async_remote_copy(
        src_ref=downward, dst_ref=from_upper, send_sem=psend.at[1], recv_sem=precv.at[1],
        device_id=(s - 1, g), device_id_type=MESH,
    )

    @pl.when(exists(1, 0))
    def _():
        up.start()

    @pl.when(jnp.logical_not(exists(-1, 0)))
    def _():
        from_lower[...] = jnp.zeros(from_lower.shape, F32)

    @pl.when(exists(-1, 0))
    def _():
        down.start()

    @pl.when(jnp.logical_not(exists(1, 0)))
    def _():
        from_upper[...] = jnp.zeros(from_upper.shape, F32)

    centre = plane(centre_h, centre_l)

    @pl.when(exists(-1, 0))
    def _():
        up.wait_recv()

    @pl.when(exists(1, 0))
    def _():
        down.wait_recv()

    out[...] = gelu(centre + from_lower[...] + from_upper[...]).T

    arrive(first, False)
    arrive(again, False)
    for copy in spread + crossed + forward + sent:
        copy.wait_send()

    @pl.when(exists(1, 0))
    def _():
        up.wait_send()

    @pl.when(exists(-1, 0))
    def _():
        down.wait_send()


def per_device(slabs, groups, volume, conv_fine, down_first, conv_middle, down_second, conv_coarse):
    c1, depth, height, width = volume.shape
    c2, c3, c4 = down_first.shape[4], conv_coarse.shape[3], conv_coarse.shape[4]
    half, quarter = width // 2, width // 4
    d2, h2 = depth // 2, height // 2
    part = down_second.shape[4]
    cells = groups * quarter
    vol = volume.reshape(c1 * depth * height, width)
    fine = conv_fine.reshape(27, c1, c1)
    down1 = down_first.reshape(2, 4 * c1, c2)
    middle = conv_middle.reshape(9, 3 * c2, c2)
    shard = jnp.swapaxes(down_second, 3, 4).reshape(8, part, c2)
    pairs = h2 + 1
    coarse_w = conv_coarse.reshape(9, 3 * c3, c4)
    V = pltpu.VMEM
    vmem, away = pl.BlockSpec(memory_space=pltpu.VMEM), pl.BlockSpec(memory_space=pl.ANY)
    dma = pltpu.SemaphoreType.DMA
    result = pl.pallas_call(
        functools.partial(kernel, slabs, groups),
        out_shape=jax.ShapeDtypeStruct((c4, cells), F32),
        in_specs=[vmem, vmem, away, away, vmem, away],
        out_specs=vmem,
        scratch_shapes=[
            V((depth + 2, height + 2, c1, width), F32),
            V((pairs, width, 2 * c1), F32),
            V((2, depth + 2, pairs, half, 8 * c1), BF16),
            V((3, 2, 8 * c1, 4 * c1), BF16),
            V((3, 2, 8 * c1, 4 * c1), BF16),
            V(down1.shape, F32),
            V(down1.shape, BF16),
            V(down1.shape, BF16),
            V(middle.shape, F32),
            V((3, 12 * c2, 2 * c2), BF16),
            V((3, 12 * c2, 2 * c2), BF16),
            V((d2 + 2, h2 + 2, half, c2), F32),
            V((2, d2 + 2, half, 12 * c2), BF16),
            V((h2, d2 * half, c2), F32),
            V((groups,) + shard.shape, F32),
            V(coarse_w.shape, F32),
            V((3, 3 * c3, 2 * c4), BF16),
            V((3, 3 * c3, 2 * c4), BF16),
            V((3, 3 * c3, c4), BF16),
            V((3, 3 * c3, c4), BF16),
            V((groups, quarter, c3), F32),
            V((2, cells + 2 * quarter, 3 * c3), BF16),
            V((cells, c4), F32),
            V((cells, c4), F32),
            V((cells, c4), F32),
            V((cells, c4), F32),
            dma((3,)),
            dma((8,)), dma((8,)), dma((8,)), dma((8,)),
            dma((groups,)), dma((groups,)), dma((groups,)), dma((groups,)), dma((groups,)), dma((groups,)), dma((groups,)), dma((groups,)),
            dma((2,)), dma((2,)),
        ],
        compiler_params=pltpu.CompilerParams(
            collective_id=0, has_side_effects=True, vmem_limit_bytes=60 * 1024 * 1024
        ),
    )(vol, fine, down1, middle, shard, coarse_w)
    return result.reshape(c4, 1, cells)


def solution(mesh):
    placed = (
        P(None, "slab", "grp", None),
        P(),
        P(),
        P(),
        P(None, None, None, None, "grp"),
        P(None, None, None, None, "grp"),
    )
    body = functools.partial(per_device, mesh.shape["slab"], mesh.shape["grp"])
    return jax.shard_map(
        body, mesh=mesh, in_specs=placed, out_specs=P("grp", "slab", None), check_vma=False
    )
```

```python
import functools

import jax
import jax.numpy as jnp
from jax import lax
from jax.experimental import pallas as pl
from jax.experimental.pallas import tpu as pltpu
from jax.sharding import PartitionSpec as P

MESH = pl.DeviceIdType.MESH
F32, BF16 = jnp.float32, jnp.bfloat16
WAYS = ((1, 0), (-1, 0), (0, 1), (0, -1), (1, 1), (1, -1), (-1, 1), (-1, -1))


def split(x):
    high = x.astype(BF16)
    return high, (x - high.astype(F32)).astype(BF16)


def stacked(x):
    return jnp.concatenate(split(x), axis=0)


def product(both, weights, dims=(((1,), (0,)), ((), ()))):
    dot = functools.partial(lax.dot_general, dimension_numbers=dims, preferred_element_type=F32)
    rows = both.shape[0] // 2
    wide = dot(both, weights[0])
    return wide[:rows] + wide[rows:] + dot(both[:rows], weights[1])


def plus(total, term):
    return term if total is None else total + term


def gelu(x):
    return 0.5 * x * (1.0 + lax.erf(x * (0.5**0.5)))


def beside(x, span):
    at = lax.rem(lax.broadcasted_iota(jnp.int32, x.shape, 0), span)
    before = jnp.where(at == 0, 0.0, pltpu.roll(x, 1, 0))
    after = jnp.where(at == span - 1, 0.0, pltpu.roll(x, x.shape[0] - 1, 0))
    return before, after


def kernel(
    slabs, groups,
    vol_hbm, fine_hbm, down1_hbm, middle_hbm, shard, coarse_hbm,
    out,
    vol, fine, field, pair, rows, fine_h, fine_l, down1, down1_h, down1_l, middle, middle_h, middle_l,
    second, rows2, level2, gathered, coarse_w, edges_h, edges_l, centre_h, centre_l,
    coarse, taps, upward, downward, from_lower, from_upper,
    load_sem, send1, recv1, send2, recv2, wsend, wrecv, xsend, xrecv, fsend, frecv, csend, crecv, psend, precv,
):
    s, g = lax.axis_index("slab"), lax.axis_index("grp")
    depth, height, chans, width = (field.shape[0] - 2, field.shape[1] - 2) + field.shape[2:]
    half = width // 2

    loads = [
        pltpu.make_async_copy(vol_hbm, vol, load_sem.at[3]),
        pltpu.make_async_copy(fine_hbm, fine, load_sem.at[4]),
        pltpu.make_async_copy(shard, gathered.at[g], load_sem.at[5]),
        pltpu.make_async_copy(down1_hbm, down1, load_sem.at[0]),
        pltpu.make_async_copy(middle_hbm, middle, load_sem.at[1]),
        pltpu.make_async_copy(coarse_hbm, coarse_w, load_sem.at[2]),
    ]
    for load in loads:
        load.start()

    def exists(ds, dg):
        return (s + ds >= 0) & (s + ds < slabs) & (g + dg >= 0) & (g + dg < groups)

    barrier = pltpu.get_barrier_semaphore()
    heard = jnp.int32(0)
    for ds, dg in WAYS:
        there = exists(ds, dg)
        heard = heard + there.astype(jnp.int32)

        @pl.when(there)
        def _():
            pl.semaphore_signal(barrier, inc=1, device_id=(s + ds, g + dg), device_id_type=MESH)

    for dg in range(2, groups):
        for sign in (1, -1):
            there = exists(0, sign * dg)
            heard = heard + there.astype(jnp.int32)

            @pl.when(there)
            def _():
                pl.semaphore_signal(barrier, inc=1, device_id=(s, g + sign * dg), device_id_type=MESH)

    sibling = s + 1 - 2 * lax.rem(s, 2)
    place = lax.rem(s // 2, 4)
    crossings = []
    for hop in (1, 2, 3):
        low, high = hop % 2, hop // 2
        step = low * (1 - 2 * lax.rem(place, 2)) + 2 * high * (1 - 2 * (place // 2))
        crossings.append(s + 2 * step)
    for peer in crossings:
        pl.semaphore_signal(barrier, inc=1, device_id=(peer, g), device_id_type=MESH)
    loads[0].wait()
    lines = depth * height
    for r in range(lines):
        field[1 + r // height, 1 + r % height] = vol[pl.ds(r, chans, stride=lines), :]
    pl.semaphore_wait(barrier, heard + len(crossings))

    def part(way, size, offset):
        if way == 0:
            return pl.ds(offset, size)
        return pl.ds(offset + (size - 1 if way > 0 else 0), 1)

    def landing(way, size):
        if way == 0:
            return pl.ds(1, size)
        return pl.ds(0 if way > 0 else size + 1, 1)

    def halo(src, offset, buf, sends, recvs):
        nd, nh = buf.shape[0] - 2, buf.shape[1] - 2
        copies = []
        for k, (ds, dg) in enumerate(WAYS):
            copies.append(
                pltpu.make_async_remote_copy(
                    src_ref=src.at[part(ds, nd, offset), part(dg, nh, offset)],
                    dst_ref=buf.at[landing(ds, nd), landing(dg, nh)],
                    send_sem=sends.at[k],
                    recv_sem=recvs.at[k],
                    device_id=(s + ds, g + dg),
                    device_id_type=MESH,
                )
            )

            @pl.when(exists(ds, dg))
            def _():
                copies[k].start()

            @pl.when(jnp.logical_not(exists(-ds, -dg)))
            def _():
                piece = (landing(ds, nd), landing(dg, nh))
                shape = (piece[0].size, piece[1].size) + buf.shape[2:]
                buf[piece[0], piece[1]] = jnp.zeros(shape, F32)

        return copies

    def arrive(copies, received, ways=range(len(WAYS))):
        for k in ways:
            ds, dg = WAYS[k]
            if received:
                @pl.when(exists(-ds, -dg))
                def _():
                    copies[k].wait_recv()
            else:
                @pl.when(exists(ds, dg))
                def _():
                    copies[k].wait_send()

    first = halo(field, 1, field, send1, recv1)

    taps_of = shard.shape[0]
    parity = lax.rem(s, 2)
    eighth = pl.ds(parity * 4 + place, 1)
    half_taps = pl.ds(parity * 4, 4)
    spread, crossed, forward = [], [], []
    for j in range(1, groups):
        copy = pltpu.make_async_remote_copy(
            src_ref=shard.at[eighth],
            dst_ref=gathered.at[g, eighth],
            send_sem=wsend.at[j],
            recv_sem=wrecv.at[j],
            device_id=(s, lax.rem(g + j, groups)),
            device_id_type=MESH,
        )
        copy.start()
        spread.append(copy)

    def hand_on(arrived, out_copies, piece, sends, recvs, peers):
        for j in range(1, groups):
            for copy in arrived[j - 1]:
                copy.wait_recv()
            source = lax.rem(g + groups - j, groups)
            made = []
            for k, peer in enumerate(peers):
                copy = pltpu.make_async_remote_copy(
                    src_ref=gathered.at[source, piece],
                    dst_ref=gathered.at[source, piece],
                    send_sem=sends.at[j, k],
                    recv_sem=recvs.at[j, k],
                    device_id=(peer, g),
                    device_id_type=MESH,
                )
                copy.start()
                made.append(copy)
            out_copies.append(made)

    loads[1].wait()
    blank = jnp.zeros((chans, 2 * chans), BF16)
    nothing = jnp.zeros((chans, chans), F32)
    for a in range(3):
        for b in range(3):
            for pos in range(4):
                left = fine[(a * 3 + b) * 3 + pos] if pos < 3 else nothing
                right = fine[(a * 3 + b) * 3 + pos - 1] if pos > 0 else nothing
                high, low = split(jnp.concatenate([left, right], axis=1))
                for hb in range(2):
                    p, sub = divmod(b + hb, 2)
                    spot = pl.ds((pos * 2 + sub) * chans, chans)
                    fine_h[a, p, spot, hb * 2 * chans : (hb + 1) * 2 * chans] = high
                    fine_l[a, p, spot, hb * 2 * chans : (hb + 1) * 2 * chans] = low
        for pos in range(4):
            for p, sub, hb in ((0, 0, 1), (1, 1, 0)):
                spot = pl.ds((pos * 2 + sub) * chans, chans)
                fine_h[a, p, spot, hb * 2 * chans : (hb + 1) * 2 * chans] = blank
                fine_l[a, p, spot, hb * 2 * chans : (hb + 1) * 2 * chans] = blank

    pairs = height // 2 + 1
    blocks = height // 2
    d2, h2, c2 = depth // 2, blocks, down1.shape[2]
    for load in loads[2:]:
        load.wait()
    for a in range(2):
        down1_h[a], down1_l[a] = split(down1[a])

    @pl.loop(0, 3)
    def _(a):
        for b in range(3):
            high, low = split(middle[a * 3 + b])
            for hb in range(2):
                spot = pl.ds((b + hb) * 3 * c2, 3 * c2)
                middle_h[a, spot, hb * c2 : (hb + 1) * c2] = high
                middle_l[a, spot, hb * c2 : (hb + 1) * c2] = low

    outs = coarse_w.shape[2]

    @pl.loop(0, 3)
    def _(b):
        for a, k in ((0, 0), (2, 1)):
            high, low = split(coarse_w[a * 3 + b])
            edges_h[b, :, k * outs : (k + 1) * outs] = high
            edges_l[b, :, k * outs : (k + 1) * outs] = low
        centre_h[b], centre_l[b] = split(coarse_w[3 + b])

    def build(p):
        @pl.loop(0, depth + 2)
        def _(d):
            pair[p] = field[d, 2 * p : 2 * p + 2].reshape(2 * chans, width).T
            even = pair[p, pl.ds(0, half, stride=2), :]
            odd = pair[p, pl.ds(1, half, stride=2), :]
            before, _ = beside(odd, half)
            _, after = beside(even, half)
            rows[0, d, p], rows[1, d, p] = split(jnp.concatenate([before, even, odd, after], axis=1))

    totals = [None] * blocks

    def convolve(p):
        for a in range(3):
            lhs = rows[:, a : a + depth, p].reshape(2 * depth * half, 8 * chans)
            for block in range(blocks):
                if 0 <= p - block <= 1:
                    w = (fine_h[a, p - block], fine_l[a, p - block])
                    totals[block] = plus(totals[block], product(lhs, w))

    arrive(first, True, range(0, 2))
    for p in range(1, blocks):
        build(p)
        convolve(p)
    arrive(first, True, range(2, len(WAYS)))
    for p in (0, blocks):
        build(p)
        convolve(p)
    hand_on([[c] for c in spread], crossed, eighth, xsend, xrecv, crossings)
    ones = [gelu(t).reshape(d2, 2, half, 4 * chans) for t in totals]
    total = None
    for a in range(2):
        lhs = jnp.concatenate([o[:, a].reshape(d2 * half, 4 * chans) for o in ones], axis=0)
        total = plus(total, product(stacked(lhs), (down1_h[a], down1_l[a])))
    total = total.reshape(h2, d2, half, c2)
    for h in range(h2):
        second[1 : d2 + 1, 1 + h] = total[h]
    again = halo(second, 1, second, send2, recv2)

    def widen(h):
        @pl.loop(0, d2 + 2)
        def _(d):
            x = second[d, h]
            before, after = beside(x, half)
            spot = slice(h * 3 * c2, (h + 1) * 3 * c2)
            rows2[0, d, :, spot], rows2[1, d, :, spot] = split(jnp.concatenate([before, x, after], axis=1))

    def middle_term(a, low, high, left, right):
        lhs = rows2[:, a : a + d2, :, low:high].reshape(2 * d2 * half, high - low)
        return product(lhs, (middle_h[a, low:high, left:right], middle_l[a, low:high, left:right]))

    k3 = 3 * c2
    arrive(again, True, range(0, 2))
    for h in range(1, h2 + 1):
        widen(h)
    total, sides = None, [None, None]
    for a in range(3):
        total = plus(total, middle_term(a, k3, 3 * k3, 0, 2 * c2))
    arrive(again, True, range(2, len(WAYS)))
    for h in (0, h2 + 1):
        widen(h)
    for a in range(3):
        sides[0] = plus(sides[0], middle_term(a, 0, k3, 0, c2))
        sides[1] = plus(sides[1], middle_term(a, 3 * k3, 4 * k3, c2, 2 * c2))
    hand_on(crossed, forward, half_taps, fsend, frecv, [sibling])
    for h in range(h2):
        level2[h] = gelu(total[:, h * c2 : (h + 1) * c2] + sides[h])
    quarter = half // 2
    lhs = jnp.concatenate(
        [
            level2[h, pl.ds(d * half + c, quarter, stride=2), :]
            for d in range(d2) for h in range(h2) for c in range(2)
        ],
        axis=1,
    )
    lhs = stacked(lhs)
    for made in forward:
        made[0].wait_recv()
    weights = jnp.concatenate(
        [gathered[:, t].reshape(groups * shard.shape[1], c2) for t in range(taps_of)], axis=1
    )
    share = product(lhs, split(weights), (((1,), (1,)), ((), ())))
    coarse[pl.ds(g, 1)] = share[None]
    sent = []
    for j in range(1, groups):
        copy = pltpu.make_async_remote_copy(
            src_ref=coarse.at[g],
            dst_ref=coarse.at[g],
            send_sem=csend.at[j],
            recv_sem=crecv.at[j],
            device_id=(s, lax.rem(g + j, groups)),
            device_id_type=MESH,
        )
        copy.start()
        sent.append(copy)
    cells = groups * quarter
    edge = jnp.zeros((2, quarter, taps.shape[2]), BF16)
    taps[:, 0:quarter] = edge
    taps[:, quarter + cells : 2 * quarter + cells] = edge
    for copy in sent:
        copy.wait_recv()
    x = coarse[...].reshape(cells, coarse.shape[2])
    before, after = beside(x, quarter)
    taps[0, quarter : quarter + cells], taps[1, quarter : quarter + cells] = split(
        jnp.concatenate([before, x, after], axis=1)
    )

    def plane(high, low):
        total = None
        for b in range(3):
            lhs = taps[:, b * quarter : b * quarter + cells].reshape(2 * cells, taps.shape[2])
            total = plus(total, product(lhs, (high[b], low[b])))
        return total

    both = plane(edges_h, edges_l)
    upward[...] = both[:, :outs]
    downward[...] = both[:, outs:]
    up = pltpu.make_async_remote_copy(
        src_ref=upward, dst_ref=from_lower, send_sem=psend.at[0], recv_sem=precv.at[0],
        device_id=(s + 1, g), device_id_type=MESH,
    )
    down = pltpu.make_async_remote_copy(
        src_ref=downward, dst_ref=from_upper, send_sem=psend.at[1], recv_sem=precv.at[1],
        device_id=(s - 1, g), device_id_type=MESH,
    )

    @pl.when(exists(1, 0))
    def _():
        up.start()

    @pl.when(jnp.logical_not(exists(-1, 0)))
    def _():
        from_lower[...] = jnp.zeros(from_lower.shape, F32)

    @pl.when(exists(-1, 0))
    def _():
        down.start()

    @pl.when(jnp.logical_not(exists(1, 0)))
    def _():
        from_upper[...] = jnp.zeros(from_upper.shape, F32)

    centre = plane(centre_h, centre_l)

    @pl.when(exists(-1, 0))
    def _():
        up.wait_recv()

    @pl.when(exists(1, 0))
    def _():
        down.wait_recv()

    out[...] = gelu(centre + from_lower[...] + from_upper[...]).T

    arrive(first, False)
    arrive(again, False)
    for copy in spread + sum(crossed + forward, []) + sent:
        copy.wait_send()

    @pl.when(exists(1, 0))
    def _():
        up.wait_send()

    @pl.when(exists(-1, 0))
    def _():
        down.wait_send()


def per_device(slabs, groups, volume, conv_fine, down_first, conv_middle, down_second, conv_coarse):
    c1, depth, height, width = volume.shape
    c2, c3, c4 = down_first.shape[4], conv_coarse.shape[3], conv_coarse.shape[4]
    half, quarter = width // 2, width // 4
    d2, h2 = depth // 2, height // 2
    part = down_second.shape[4]
    cells = groups * quarter
    vol = volume.reshape(c1 * depth * height, width)
    fine = conv_fine.reshape(27, c1, c1)
    down1 = down_first.reshape(2, 4 * c1, c2)
    middle = conv_middle.reshape(9, 3 * c2, c2)
    shard = jnp.swapaxes(down_second, 3, 4).reshape(8, part, c2)
    pairs = h2 + 1
    coarse_w = conv_coarse.reshape(9, 3 * c3, c4)
    V = pltpu.VMEM
    vmem, away = pl.BlockSpec(memory_space=pltpu.VMEM), pl.BlockSpec(memory_space=pl.ANY)
    dma = pltpu.SemaphoreType.DMA
    result = pl.pallas_call(
        functools.partial(kernel, slabs, groups),
        out_shape=jax.ShapeDtypeStruct((c4, cells), F32),
        in_specs=[away] * 6,
        out_specs=vmem,
        scratch_shapes=[
            V(vol.shape, F32),
            V(fine.shape, F32),
            V((depth + 2, height + 2, c1, width), F32),
            V((pairs, width, 2 * c1), F32),
            V((2, depth + 2, pairs, half, 8 * c1), BF16),
            V((3, 2, 8 * c1, 4 * c1), BF16),
            V((3, 2, 8 * c1, 4 * c1), BF16),
            V(down1.shape, F32),
            V(down1.shape, BF16),
            V(down1.shape, BF16),
            V(middle.shape, F32),
            V((3, 12 * c2, 2 * c2), BF16),
            V((3, 12 * c2, 2 * c2), BF16),
            V((d2 + 2, h2 + 2, half, c2), F32),
            V((2, d2 + 2, half, 12 * c2), BF16),
            V((h2, d2 * half, c2), F32),
            V((groups,) + shard.shape, F32),
            V(coarse_w.shape, F32),
            V((3, 3 * c3, 2 * c4), BF16),
            V((3, 3 * c3, 2 * c4), BF16),
            V((3, 3 * c3, c4), BF16),
            V((3, 3 * c3, c4), BF16),
            V((groups, quarter, c3), F32),
            V((2, cells + 2 * quarter, 3 * c3), BF16),
            V((cells, c4), F32),
            V((cells, c4), F32),
            V((cells, c4), F32),
            V((cells, c4), F32),
            dma((6,)),
            dma((8,)), dma((8,)), dma((8,)), dma((8,)),
            dma((groups,)), dma((groups,)), dma((groups, 3)), dma((groups, 3)), dma((groups, 1)), dma((groups, 1)), dma((groups,)), dma((groups,)),
            dma((2,)), dma((2,)),
        ],
        compiler_params=pltpu.CompilerParams(
            collective_id=0, has_side_effects=True, vmem_limit_bytes=60 * 1024 * 1024
        ),
    )(vol, fine, down1, middle, shard, coarse_w)
    return result.reshape(c4, 1, cells)


def solution(mesh):
    placed = (
        P(None, "slab", "grp", None),
        P(),
        P(),
        P(),
        P(None, None, None, None, "grp"),
        P(None, None, None, None, "grp"),
    )
    body = functools.partial(per_device, mesh.shape["slab"], mesh.shape["grp"])
    return jax.shard_map(
        body, mesh=mesh, in_specs=placed, out_specs=P("grp", "slab", None), check_vma=False
    )
```

```python
import functools

import jax
import jax.numpy as jnp
from jax import lax
from jax.experimental import pallas as pl
from jax.experimental.pallas import tpu as pltpu
from jax.sharding import PartitionSpec as P

MESH = pl.DeviceIdType.MESH
F32, BF16 = jnp.float32, jnp.bfloat16
WAYS = ((1, 0), (-1, 0), (0, 1), (0, -1), (1, 1), (1, -1), (-1, 1), (-1, -1))


def split(x):
    high = x.astype(BF16)
    return high, (x - high.astype(F32)).astype(BF16)


def stacked(x):
    return jnp.concatenate(split(x), axis=0)


def product(both, weights, dims=(((1,), (0,)), ((), ()))):
    dot = functools.partial(lax.dot_general, dimension_numbers=dims, preferred_element_type=F32)
    rows = both.shape[0] // 2
    wide = dot(both, weights[0])
    return wide[:rows] + wide[rows:] + dot(both[:rows], weights[1])


def plus(total, term):
    return term if total is None else total + term


def gelu(x):
    return 0.5 * x * (1.0 + lax.erf(x * (0.5**0.5)))


def beside(x, span):
    at = lax.rem(lax.broadcasted_iota(jnp.int32, x.shape, 0), span)
    before = jnp.where(at == 0, 0.0, pltpu.roll(x, 1, 0))
    after = jnp.where(at == span - 1, 0.0, pltpu.roll(x, x.shape[0] - 1, 0))
    return before, after


def kernel(
    slabs, groups,
    vol_hbm, fine_hbm, down1_hbm, middle_hbm, shard, coarse_hbm,
    out,
    vol, fine, field, pair, rows, fine_h, fine_l, down1, down1_h, down1_l, middle, middle_h, middle_l,
    second, rows2, level2, gathered, coarse_w, edges_h, edges_l, centre_h, centre_l,
    coarse, taps, upward, downward, from_lower, from_upper,
    load_sem, send1, recv1, send2, recv2, wsend, wrecv, xsend, xrecv, fsend, frecv, csend, crecv, psend, precv,
):
    s, g = lax.axis_index("slab"), lax.axis_index("grp")
    depth, height, chans, width = (field.shape[0] - 2, field.shape[1] - 2) + field.shape[2:]
    half = width // 2

    loads = [
        pltpu.make_async_copy(vol_hbm, vol, load_sem.at[3]),
        pltpu.make_async_copy(fine_hbm, fine, load_sem.at[4]),
        pltpu.make_async_copy(shard, gathered.at[g], load_sem.at[5]),
        pltpu.make_async_copy(down1_hbm, down1, load_sem.at[0]),
        pltpu.make_async_copy(middle_hbm, middle, load_sem.at[1]),
        pltpu.make_async_copy(coarse_hbm, coarse_w, load_sem.at[2]),
    ]
    for load in loads:
        load.start()

    def exists(ds, dg):
        return (s + ds >= 0) & (s + ds < slabs) & (g + dg >= 0) & (g + dg < groups)

    barrier = pltpu.get_barrier_semaphore()
    heard = jnp.int32(0)
    for ds, dg in WAYS:
        there = exists(ds, dg)
        heard = heard + there.astype(jnp.int32)

        @pl.when(there)
        def _():
            pl.semaphore_signal(barrier, inc=1, device_id=(s + ds, g + dg), device_id_type=MESH)

    for dg in range(2, groups):
        for sign in (1, -1):
            there = exists(0, sign * dg)
            heard = heard + there.astype(jnp.int32)

            @pl.when(there)
            def _():
                pl.semaphore_signal(barrier, inc=1, device_id=(s, g + sign * dg), device_id_type=MESH)

    sibling = s + 1 - 2 * lax.rem(s, 2)
    place = lax.rem(s // 2, 2)
    crossings = [s + 2 - 4 * place]
    for peer in crossings:
        pl.semaphore_signal(barrier, inc=1, device_id=(peer, g), device_id_type=MESH)
    loads[0].wait()
    lines = depth * height
    for r in range(lines):
        field[1 + r // height, 1 + r % height] = vol[pl.ds(r, chans, stride=lines), :]
    pl.semaphore_wait(barrier, heard + len(crossings))

    def part(way, size, offset):
        if way == 0:
            return pl.ds(offset, size)
        return pl.ds(offset + (size - 1 if way > 0 else 0), 1)

    def landing(way, size):
        if way == 0:
            return pl.ds(1, size)
        return pl.ds(0 if way > 0 else size + 1, 1)

    def halo(src, offset, buf, sends, recvs):
        nd, nh = buf.shape[0] - 2, buf.shape[1] - 2
        copies = []
        for k, (ds, dg) in enumerate(WAYS):
            copies.append(
                pltpu.make_async_remote_copy(
                    src_ref=src.at[part(ds, nd, offset), part(dg, nh, offset)],
                    dst_ref=buf.at[landing(ds, nd), landing(dg, nh)],
                    send_sem=sends.at[k],
                    recv_sem=recvs.at[k],
                    device_id=(s + ds, g + dg),
                    device_id_type=MESH,
                )
            )

            @pl.when(exists(ds, dg))
            def _():
                copies[k].start()

            @pl.when(jnp.logical_not(exists(-ds, -dg)))
            def _():
                piece = (landing(ds, nd), landing(dg, nh))
                shape = (piece[0].size, piece[1].size) + buf.shape[2:]
                buf[piece[0], piece[1]] = jnp.zeros(shape, F32)

        return copies

    def arrive(copies, received, ways=range(len(WAYS))):
        for k in ways:
            ds, dg = WAYS[k]
            if received:
                @pl.when(exists(-ds, -dg))
                def _():
                    copies[k].wait_recv()
            else:
                @pl.when(exists(ds, dg))
                def _():
                    copies[k].wait_send()

    first = halo(field, 1, field, send1, recv1)

    taps_of = shard.shape[0]
    parity = lax.rem(s, 2)
    fourth = pl.ds((parity * 2 + place) * (taps_of // 4), taps_of // 4)
    half_taps = pl.ds(parity * (taps_of // 2), taps_of // 2)
    spread, crossed, forward = [], [], []
    for j in range(1, groups):
        copy = pltpu.make_async_remote_copy(
            src_ref=shard.at[fourth],
            dst_ref=gathered.at[g, fourth],
            send_sem=wsend.at[j],
            recv_sem=wrecv.at[j],
            device_id=(s, lax.rem(g + j, groups)),
            device_id_type=MESH,
        )
        copy.start()
        spread.append(copy)

    def hand_on(arrived, out_copies, piece, sends, recvs, peers):
        for j in range(1, groups):
            for copy in arrived[j - 1]:
                copy.wait_recv()
            source = lax.rem(g + groups - j, groups)
            made = []
            for k, peer in enumerate(peers):
                copy = pltpu.make_async_remote_copy(
                    src_ref=gathered.at[source, piece],
                    dst_ref=gathered.at[source, piece],
                    send_sem=sends.at[j, k],
                    recv_sem=recvs.at[j, k],
                    device_id=(peer, g),
                    device_id_type=MESH,
                )
                copy.start()
                made.append(copy)
            out_copies.append(made)

    loads[1].wait()
    blank = jnp.zeros((chans, 2 * chans), BF16)
    nothing = jnp.zeros((chans, chans), F32)
    for a in range(3):
        for b in range(3):
            for pos in range(4):
                left = fine[(a * 3 + b) * 3 + pos] if pos < 3 else nothing
                right = fine[(a * 3 + b) * 3 + pos - 1] if pos > 0 else nothing
                high, low = split(jnp.concatenate([left, right], axis=1))
                for hb in range(2):
                    p, sub = divmod(b + hb, 2)
                    spot = pl.ds((pos * 2 + sub) * chans, chans)
                    fine_h[a, p, spot, hb * 2 * chans : (hb + 1) * 2 * chans] = high
                    fine_l[a, p, spot, hb * 2 * chans : (hb + 1) * 2 * chans] = low
        for pos in range(4):
            for p, sub, hb in ((0, 0, 1), (1, 1, 0)):
                spot = pl.ds((pos * 2 + sub) * chans, chans)
                fine_h[a, p, spot, hb * 2 * chans : (hb + 1) * 2 * chans] = blank
                fine_l[a, p, spot, hb * 2 * chans : (hb + 1) * 2 * chans] = blank

    pairs = height // 2 + 1
    blocks = height // 2
    d2, h2, c2 = depth // 2, blocks, down1.shape[2]
    for load in loads[2:]:
        load.wait()
    for a in range(2):
        down1_h[a], down1_l[a] = split(down1[a])

    @pl.loop(0, 3)
    def _(a):
        for b in range(3):
            high, low = split(middle[a * 3 + b])
            for hb in range(2):
                spot = pl.ds((b + hb) * 3 * c2, 3 * c2)
                middle_h[a, spot, hb * c2 : (hb + 1) * c2] = high
                middle_l[a, spot, hb * c2 : (hb + 1) * c2] = low

    outs = coarse_w.shape[2]

    @pl.loop(0, 3)
    def _(b):
        for a, k in ((0, 0), (2, 1)):
            high, low = split(coarse_w[a * 3 + b])
            edges_h[b, :, k * outs : (k + 1) * outs] = high
            edges_l[b, :, k * outs : (k + 1) * outs] = low
        centre_h[b], centre_l[b] = split(coarse_w[3 + b])

    def build(p):
        @pl.loop(0, depth + 2)
        def _(d):
            pair[p] = field[d, 2 * p : 2 * p + 2].reshape(2 * chans, width).T
            even = pair[p, pl.ds(0, half, stride=2), :]
            odd = pair[p, pl.ds(1, half, stride=2), :]
            before, _ = beside(odd, half)
            _, after = beside(even, half)
            rows[0, d, p], rows[1, d, p] = split(jnp.concatenate([before, even, odd, after], axis=1))

    totals = [None] * blocks

    def convolve(p):
        for a in range(3):
            lhs = rows[:, a : a + depth, p].reshape(2 * depth * half, 8 * chans)
            for block in range(blocks):
                if 0 <= p - block <= 1:
                    w = (fine_h[a, p - block], fine_l[a, p - block])
                    totals[block] = plus(totals[block], product(lhs, w))

    arrive(first, True, range(0, 2))
    for p in range(1, blocks):
        build(p)
        convolve(p)
    arrive(first, True, range(2, len(WAYS)))
    for p in (0, blocks):
        build(p)
        convolve(p)
    ones = [gelu(t).reshape(d2, 2, half, 4 * chans) for t in totals]
    total = None
    for a in range(2):
        lhs = jnp.concatenate([o[:, a].reshape(d2 * half, 4 * chans) for o in ones], axis=0)
        total = plus(total, product(stacked(lhs), (down1_h[a], down1_l[a])))
    total = total.reshape(h2, d2, half, c2)
    for h in range(h2):
        second[1 : d2 + 1, 1 + h] = total[h]
    again = halo(second, 1, second, send2, recv2)
    hand_on([[c] for c in spread], crossed, fourth, xsend, xrecv, crossings)

    def widen(h):
        @pl.loop(0, d2 + 2)
        def _(d):
            x = second[d, h]
            before, after = beside(x, half)
            spot = slice(h * 3 * c2, (h + 1) * 3 * c2)
            rows2[0, d, :, spot], rows2[1, d, :, spot] = split(jnp.concatenate([before, x, after], axis=1))

    def middle_term(a, low, high, left, right):
        lhs = rows2[:, a : a + d2, :, low:high].reshape(2 * d2 * half, high - low)
        return product(lhs, (middle_h[a, low:high, left:right], middle_l[a, low:high, left:right]))

    k3 = 3 * c2
    arrive(again, True, range(0, 2))
    for h in range(1, h2 + 1):
        widen(h)
    total, sides = None, [None, None]
    for a in range(3):
        total = plus(total, middle_term(a, k3, 3 * k3, 0, 2 * c2))
    arrive(again, True, range(2, len(WAYS)))
    for h in (0, h2 + 1):
        widen(h)
    for a in range(3):
        sides[0] = plus(sides[0], middle_term(a, 0, k3, 0, c2))
        sides[1] = plus(sides[1], middle_term(a, 3 * k3, 4 * k3, c2, 2 * c2))
    hand_on(crossed, forward, half_taps, fsend, frecv, [sibling])
    for h in range(h2):
        level2[h] = gelu(total[:, h * c2 : (h + 1) * c2] + sides[h])
    quarter = half // 2
    lhs = jnp.concatenate(
        [
            level2[h, pl.ds(d * half + c, quarter, stride=2), :]
            for d in range(d2) for h in range(h2) for c in range(2)
        ],
        axis=1,
    )
    lhs = stacked(lhs)
    for made in forward:
        made[0].wait_recv()
    weights = jnp.concatenate(
        [gathered[:, t].reshape(groups * shard.shape[1], c2) for t in range(taps_of)], axis=1
    )
    share = product(lhs, split(weights), (((1,), (1,)), ((), ())))
    coarse[pl.ds(g, 1)] = share[None]
    sent = []
    for j in range(1, groups):
        copy = pltpu.make_async_remote_copy(
            src_ref=coarse.at[g],
            dst_ref=coarse.at[g],
            send_sem=csend.at[j],
            recv_sem=crecv.at[j],
            device_id=(s, lax.rem(g + j, groups)),
            device_id_type=MESH,
        )
        copy.start()
        sent.append(copy)
    cells = groups * quarter
    edge = jnp.zeros((2, quarter, taps.shape[2]), BF16)
    taps[:, 0:quarter] = edge
    taps[:, quarter + cells : 2 * quarter + cells] = edge
    for copy in sent:
        copy.wait_recv()
    x = coarse[...].reshape(cells, coarse.shape[2])
    before, after = beside(x, quarter)
    taps[0, quarter : quarter + cells], taps[1, quarter : quarter + cells] = split(
        jnp.concatenate([before, x, after], axis=1)
    )

    def plane(high, low):
        total = None
        for b in range(3):
            lhs = taps[:, b * quarter : b * quarter + cells].reshape(2 * cells, taps.shape[2])
            total = plus(total, product(lhs, (high[b], low[b])))
        return total

    both = plane(edges_h, edges_l)
    upward[...] = both[:, :outs]
    downward[...] = both[:, outs:]
    up = pltpu.make_async_remote_copy(
        src_ref=upward, dst_ref=from_lower, send_sem=psend.at[0], recv_sem=precv.at[0],
        device_id=(s + 1, g), device_id_type=MESH,
    )
    down = pltpu.make_async_remote_copy(
        src_ref=downward, dst_ref=from_upper, send_sem=psend.at[1], recv_sem=precv.at[1],
        device_id=(s - 1, g), device_id_type=MESH,
    )

    @pl.when(exists(1, 0))
    def _():
        up.start()

    @pl.when(jnp.logical_not(exists(-1, 0)))
    def _():
        from_lower[...] = jnp.zeros(from_lower.shape, F32)

    @pl.when(exists(-1, 0))
    def _():
        down.start()

    @pl.when(jnp.logical_not(exists(1, 0)))
    def _():
        from_upper[...] = jnp.zeros(from_upper.shape, F32)

    centre = plane(centre_h, centre_l)

    @pl.when(exists(-1, 0))
    def _():
        up.wait_recv()

    @pl.when(exists(1, 0))
    def _():
        down.wait_recv()

    out[...] = gelu(centre + from_lower[...] + from_upper[...]).T

    arrive(first, False)
    arrive(again, False)
    for copy in spread + sum(crossed + forward, []) + sent:
        copy.wait_send()

    @pl.when(exists(1, 0))
    def _():
        up.wait_send()

    @pl.when(exists(-1, 0))
    def _():
        down.wait_send()


def per_device(slabs, groups, volume, conv_fine, down_first, conv_middle, down_second, conv_coarse):
    c1, depth, height, width = volume.shape
    c2, c3, c4 = down_first.shape[4], conv_coarse.shape[3], conv_coarse.shape[4]
    half, quarter = width // 2, width // 4
    d2, h2 = depth // 2, height // 2
    part = down_second.shape[4]
    cells = groups * quarter
    vol = volume.reshape(c1 * depth * height, width)
    fine = conv_fine.reshape(27, c1, c1)
    down1 = down_first.reshape(2, 4 * c1, c2)
    middle = conv_middle.reshape(9, 3 * c2, c2)
    shard = jnp.swapaxes(down_second, 3, 4).reshape(8, part, c2)
    pairs = h2 + 1
    coarse_w = conv_coarse.reshape(9, 3 * c3, c4)
    V = pltpu.VMEM
    vmem, away = pl.BlockSpec(memory_space=pltpu.VMEM), pl.BlockSpec(memory_space=pl.ANY)
    dma = pltpu.SemaphoreType.DMA
    result = pl.pallas_call(
        functools.partial(kernel, slabs, groups),
        out_shape=jax.ShapeDtypeStruct((c4, cells), F32),
        in_specs=[away] * 6,
        out_specs=vmem,
        scratch_shapes=[
            V(vol.shape, F32),
            V(fine.shape, F32),
            V((depth + 2, height + 2, c1, width), F32),
            V((pairs, width, 2 * c1), F32),
            V((2, depth + 2, pairs, half, 8 * c1), BF16),
            V((3, 2, 8 * c1, 4 * c1), BF16),
            V((3, 2, 8 * c1, 4 * c1), BF16),
            V(down1.shape, F32),
            V(down1.shape, BF16),
            V(down1.shape, BF16),
            V(middle.shape, F32),
            V((3, 12 * c2, 2 * c2), BF16),
            V((3, 12 * c2, 2 * c2), BF16),
            V((d2 + 2, h2 + 2, half, c2), F32),
            V((2, d2 + 2, half, 12 * c2), BF16),
            V((h2, d2 * half, c2), F32),
            V((groups,) + shard.shape, F32),
            V(coarse_w.shape, F32),
            V((3, 3 * c3, 2 * c4), BF16),
            V((3, 3 * c3, 2 * c4), BF16),
            V((3, 3 * c3, c4), BF16),
            V((3, 3 * c3, c4), BF16),
            V((groups, quarter, c3), F32),
            V((2, cells + 2 * quarter, 3 * c3), BF16),
            V((cells, c4), F32),
            V((cells, c4), F32),
            V((cells, c4), F32),
            V((cells, c4), F32),
            dma((6,)),
            dma((8,)), dma((8,)), dma((8,)), dma((8,)),
            dma((groups,)), dma((groups,)), dma((groups, 3)), dma((groups, 3)), dma((groups, 1)), dma((groups, 1)), dma((groups,)), dma((groups,)),
            dma((2,)), dma((2,)),
        ],
        compiler_params=pltpu.CompilerParams(
            collective_id=0, has_side_effects=True, vmem_limit_bytes=60 * 1024 * 1024
        ),
    )(vol, fine, down1, middle, shard, coarse_w)
    return result.reshape(c4, 1, cells)


def solution(mesh):
    placed = (
        P(None, "slab", "grp", None),
        P(),
        P(),
        P(),
        P(None, None, None, None, "grp"),
        P(None, None, None, None, "grp"),
    )
    body = functools.partial(per_device, mesh.shape["slab"], mesh.shape["grp"])
    return jax.shard_map(
        body, mesh=mesh, in_specs=placed, out_specs=P("grp", "slab", None), check_vma=False
    )
```
